32 devices in a mesh: dp: 8 (over z, y), tensor: 4 (over x, core).
Axes of the slice: x: 2, y: 2, z: 4, core: 2. Of those that a mesh axis runs over, the one named last changes fastest.
Arguments:
- attn_out: bfloat16 [1280, 2048], P('dp', 'tensor'), may hold values from -6 to 6
- residual: bfloat16 [1280, 2048], P(('dp', 'tensor')), may hold values from -6 to 6
- out_weight: bfloat16 [2048, 2048], P('tensor'), may hold values from -0.125 to 0.125
- norm_gain: float32 [2048], replicated, may hold values from 0.25 to 1.75
- router_weight: bfloat16 [2048, 64], replicated, may hold values from -0.125 to 0.125
- routes: int32 [1280, 8], P(('dp', 'tensor')), may hold values from 0 to 63, all different within a row; in each aligned block of 40 rows (0 to 39, 40 to 79, ...) at most 8 rows name the same one
- gate_up: bfloat16 [64, 2048, 2, 1024], P('dp', None, None, 'tensor'), may hold values from -0.125 to 0.125
- down_weight: bfloat16 [64, 1024, 2048], P('dp', 'tensor'), may hold values from -0.1875 to 0.1875
- final_gain: float32 [2048], replicated, may hold values from 0.25 to 1.75
- kv_pages: bfloat16 [256, 16, 16, 256], P('dp', None, 'tensor'), may hold values from -6 to 6
- page_pick: int32 [8, 2], P('dp'), may hold values from 0 to 31
- destination: int32 [8, 2], P('dp'), may hold values from 0 to 7, as said below
Outputs:
- new_residual: bfloat16 [1280, 2048], P(('dp', 'tensor'))
- normed: bfloat16 [1280, 2048], P(('dp', 'tensor'))
- arrived: bfloat16 [16, 16, 16, 256], P('dp', None, 'tensor')
The draws below stay inside these ranges and needn't reach their ends.
Inputs may be any that keep to these rules, and one draw needn't show every extreme that they name: `routes`: each row names 8 different experts; within the rows of one device (aligned blocks of 40 rows) no expert is named by more than 8 rows. `destination`: each column is a permutation of the indices of dp.
All inputs are finite; a program needn't handle non-finite values.
Results may differ from the reference program's by a relative error of at most 0.02.
Values may be sent and summed in bfloat16 or wider, within the bound.
A program may use at most 192 MiB of HBM per device.

```python
import math
import jax
import jax.numpy as jnp
import numpy as np
from jax import lax

D = 2048
HEADS = 16
HD = 128
EXPERTS = 64
FF = 1024
TOPK = 8
TOKQ = 40
CAP = 8
PAGE = 16
PAGES = 32
MIG = 2
TOKENS = 1280
N_DP = 8
N_TENSOR = 4


def force_entry(column, source, target):
    iota = jnp.arange(N_DP, dtype=jnp.int32)
    current = jnp.sum(jnp.where(iota == source, column, 0)).astype(jnp.int32)
    column = jnp.where(column == target, current, column)
    column = jnp.where(iota == source, target, column)
    return column.astype(jnp.int32)


def draw_destination(key, part):
    columns = []
    for slot_number in range(MIG):
        column = jax.random.permutation(jax.random.fold_in(key, 11 + slot_number), N_DP).astype(jnp.int32)
        start = jax.random.randint(jax.random.fold_in(key, 101 + slot_number), (), 0, N_DP).astype(jnp.int32)
        if slot_number % 2 == 0:
            column = force_entry(column, start, (start + N_DP // 2) % N_DP)
        else:
            column = force_entry(column, start, (start + 1) % N_DP)
            column = force_entry(column, (start + 3) % N_DP, (start + 2) % N_DP)
        columns.append(column)
    return jnp.stack(columns, axis=1).astype(jnp.int32)


def place_ends(entries, stream_key, smallest, high):
    longest = entries.shape.index(max(entries.shape))
    spots = []
    for shift in (0, 1):
        where = [jax.random.randint(jax.random.fold_in(stream_key, axis), (), 0, length) for axis, length in enumerate(entries.shape)]
        where[longest] = (where[longest] + shift) % entries.shape[longest]
        spots.append(tuple(where))
    return entries.at[spots[0]].set(smallest).at[spots[1]].set(high)


def shard_levels(key, shape, split, least, top_value):
    gain, own = 1.0, jax.random.fold_in(key, 6)
    for position, parts in split:
        draws = jnp.exp(jax.random.uniform(jax.random.fold_in(own, position), (parts,), jnp.float32, least / len(split), top_value / len(split)))
        gain = gain * jnp.repeat(draws, shape[position] // parts).reshape([-1 if axis == position else 1 for axis in range(len(shape))])
    return gain


def assign_block(rng, own, number, rows, count, top, bound, lean):
    ranking = jax.random.permutation(rng, count)
    heavy_load, common = load_shares(count, rows * top, bound, lean, True), load_shares(count, rows * top, bound, lean, False)
    places = jnp.arange(count)

    def named(lengths, rotation):
        used = int((lengths > 0).sum())
        fixed = max(1, used // 4)
        moved = fixed + (places - fixed + rotation * (used - fixed)) % max(1, count - fixed)
        return jnp.zeros((count,), jnp.int32).at[ranking[jnp.where(places < fixed, places, moved)]].set(jnp.asarray(lengths, jnp.int32))

    lengths = jnp.where(number % 4 == 0, named(heavy_load, number // 4), named(common, number - number // 4 - 1))
    mixed = jax.random.permutation(jax.random.fold_in(own, 3), count)
    donor, taker = mixed[0:count // 2 * 2:2], mixed[1:count // 2 * 2:2]
    room = jnp.minimum(lengths[donor] - 1, bound - lengths[taker]) // 2
    room = jnp.where((donor == ranking[0]) | (taker == ranking[0]) | (lengths[taker] == 0), 0, jnp.maximum(room, 0))
    moved = jax.random.randint(jax.random.fold_in(own, 4), (count // 2,), 0, 1 << 20) % (room + 1)
    lengths = lengths.at[donor].add(-moved).at[taker].add(moved)
    labels = jnp.searchsorted(jnp.cumsum(lengths), jnp.arange(rows * top), side="right").astype(jnp.int32)
    listing = labels.reshape(top, rows).T
    listing = listing[jax.random.permutation(jax.random.fold_in(own, 1), rows)]
    rotation = jax.random.randint(jax.random.fold_in(own, 2), (rows, 1), 0, top)
    return jnp.take_along_axis(listing, (jnp.arange(top)[None, :] + rotation) % top, axis=1)


def load_shares(amount, total, bound, skew, full):
    weights = [(1 << 20) // math.isqrt(grade ** skew) + 1 for grade in range(1, amount + 1)]
    largest = bound if full else min(bound, max(-(-total // amount), total * weights[0] // sum(weights)))
    least = 1 if total - largest >= amount - 1 else 0
    holding, rest = [largest] + [least] * (amount - 1), total - largest - least * (amount - 1)
    while rest > 0:
        candidates = [i for i in range(1, amount) if holding[i] < largest] or [i for i in range(1, amount) if holding[i] < bound]
        mass, budget = sum([weights[i] for i in candidates]), rest
        for i in candidates:
            more = min(bound - holding[i], max(1, budget * weights[i] // mass), rest)
            holding[i] = holding[i] + more
            rest = rest - more
    return np.array(holding)


def normal_values(stream_key, dims, deviation, reach, cuts=(), held_as=jnp.bfloat16):
    factor_of = shard_levels(stream_key, dims, cuts, -0.22, 0.18) if cuts else 1.0
    result = jax.random.normal(stream_key, dims, jnp.float32) * deviation * factor_of
    return jnp.minimum(jnp.maximum(result, -reach), reach).astype(held_as)


def setup_inputs(seed: int = 0) -> dict:
    key_of = jax.random.split(jax.random.key(seed), 13)
    attn_out = normal_values(key_of[0], (TOKENS, HEADS * HD), 1.0, 6.0, ((0, 8), (1, 4)))
    residual = normal_values(key_of[1], (TOKENS, D), 1.0, 6.0, ((0, 32),))
    out_weight = normal_values(key_of[2], (HEADS * HD, D), (HEADS * HD) ** -0.5, 0.125, ((0, 4),))
    norm_gain = jnp.clip(1.0 + 0.15 * jax.random.normal(key_of[3], (D,), jnp.float32), 0.25, 1.75)
    router_weight = normal_values(key_of[4], (D, EXPERTS), D ** -0.5, 0.125)
    routes_keys = jax.random.split(jax.random.fold_in(key_of[5], 1), TOKENS // TOKQ)
    routes_turns = jax.random.permutation(jax.random.fold_in(key_of[5], 3), TOKENS // TOKQ)
    routes = jax.vmap(lambda own, number: assign_block(jax.random.fold_in(key_of[5], 2), own, number, TOKQ, EXPERTS, TOPK, CAP, 2))(routes_keys, routes_turns).reshape((TOKENS, TOPK))
    gate_up = normal_values(key_of[6], (EXPERTS, D, 2, FF), D ** -0.5, 0.125, ((0, 8), (3, 4)))
    down_weight = normal_values(key_of[7], (EXPERTS, FF, D), FF ** -0.5, 0.1875, ((0, 8), (1, 4)))
    final_gain = jnp.clip(1.0 + 0.15 * jax.random.normal(key_of[8], (D,), jnp.float32), 0.25, 1.75)
    kv_pages = normal_values(key_of[9], (N_DP * PAGES, PAGE, HEADS, 2 * HD), 1.0, 6.0, ((0, 8), (2, 4)))
    page_pick = place_ends(jax.random.randint(key_of[10], (N_DP, MIG), 0, PAGES), jax.random.fold_in(key_of[10], 1), 0, PAGES - 1).astype(jnp.int32)
    destination = draw_destination(jax.random.fold_in(key_of[12], 71), 0)
    return dict(attn_out=attn_out, residual=residual, out_weight=out_weight, norm_gain=norm_gain, router_weight=router_weight, routes=routes, gate_up=gate_up, down_weight=down_weight, final_gain=final_gain, kv_pages=kv_pages, page_pick=page_pick, destination=destination)


def rms_scale(values, gain_vec):
    mean_sq = lax.optimization_barrier(jnp.mean(values * values, axis=-1, keepdims=True))
    return values * lax.rsqrt(mean_sq + 1e-06) * gain_vec

def reference(attn_out, residual, out_weight, norm_gain, router_weight, routes, gate_up, down_weight, final_gain, kv_pages, page_pick, destination):
    projected = jnp.dot(attn_out, out_weight, preferred_element_type=jnp.float32)
    mixed_sum = residual.astype(jnp.float32) + projected
    normed_in = rms_scale(mixed_sum, norm_gain).astype(jnp.bfloat16)
    logits = jnp.dot(normed_in, router_weight, preferred_element_type=jnp.float32)
    picked = jnp.take_along_axis(logits, routes, axis=1)
    gate_values = jax.nn.sigmoid(picked).astype(jnp.bfloat16)
    expert_iota = jnp.arange(EXPERTS, dtype=jnp.int32)
    onehot = (routes[:, :, None] == expert_iota[None, None, :]).astype(jnp.float32)
    gate_table = jnp.einsum('tk,tke->te', gate_values.astype(jnp.float32), onehot)
    most_rows = min(TOKENS, N_DP * N_TENSOR * CAP)
    row_iota = jnp.arange(most_rows, dtype=jnp.int32)

    def one_expert(running, inputs):
        expert_index, paired_weight, down_mat = inputs
        routed = jnp.any(routes == expert_index, axis=1)
        routed_count = jnp.sum(routed.astype(jnp.int32))
        positions = jnp.nonzero(routed, size=most_rows, fill_value=0)[0].astype(jnp.int32)
        valid = (row_iota < routed_count).astype(jnp.float32)
        weight = gate_table[positions, expert_index] * valid
        expert_rows = normed_in[positions].astype(jnp.float32)
        paired = jnp.einsum('md,dgf->mgf', expert_rows, paired_weight.astype(jnp.float32))
        hidden = (jax.nn.silu(paired[:, 0, :]) * paired[:, 1, :]).astype(jnp.bfloat16)
        expert_out = jnp.dot(hidden, down_mat, preferred_element_type=jnp.float32).astype(jnp.bfloat16)
        running = running.at[positions].add(weight[:, None] * expert_out.astype(jnp.float32))
        return (running, None)
    initial = jnp.zeros((TOKENS, D), jnp.float32)
    moe_sum, _ = lax.scan(one_expert, initial, (expert_iota, gate_up, down_weight))
    combined = mixed_sum + moe_sum
    new_residual = combined.astype(jnp.bfloat16)
    normed = rms_scale(combined, final_gain).astype(jnp.bfloat16)
    slot_iota = jnp.arange(MIG, dtype=jnp.int32)
    sources = (jnp.arange(N_DP, dtype=jnp.int32)[:, None] * PAGES + page_pick).reshape(-1).astype(jnp.int32)
    targets = (destination * MIG + slot_iota[None, :]).reshape(-1).astype(jnp.int32)
    arrived = jnp.zeros((N_DP * MIG,) + kv_pages.shape[1:], kv_pages.dtype).at[targets].set(kv_pages[sources])
    return (new_residual, normed, arrived)
```

```python
import jax
import jax.numpy as jnp
from jax import lax
from jax.sharding import PartitionSpec as P

CAP = 8


def rms_scale(values, gain_vec):
    mean_sq = jnp.mean(values * values, axis=-1, keepdims=True)
    return values * lax.rsqrt(mean_sq + 1e-06) * gain_vec


def migrate(kv_pages, page_pick, destination):
    groups = lax.axis_size("dp")
    chosen_pages = kv_pages[page_pick[0]]
    owners = jnp.arange(groups, dtype=jnp.int32)[:, None] == destination[0][None, :]
    outgoing = jnp.where(
        owners[:, :, None, None, None], chosen_pages[None], jnp.zeros((), kv_pages.dtype)
    )
    incoming = lax.all_to_all(outgoing, "dp", split_axis=0, concat_axis=0, tiled=True)
    return jnp.sum(incoming, axis=0)


def local_slots(routes_all, first, local_experts, groups, shards, rows):
    hits = jnp.any(
        routes_all[:, :, None] == first + jnp.arange(local_experts, dtype=jnp.int32), axis=1
    )
    hits = hits.reshape(groups, shards * rows, local_experts)
    token = jnp.arange(shards * rows, dtype=jnp.int32)
    before = (token[:, None] > token[None, :]) & (
        token[:, None] // rows == token[None, :] // rows
    )
    rank = jnp.einsum(
        "ut,bte->bue",
        before.astype(jnp.bfloat16),
        hits.astype(jnp.bfloat16),
        preferred_element_type=jnp.float32,
    ).astype(jnp.int32)
    within = (token // rows * CAP)[None, :, None] + rank
    within = jnp.where(hits, within, -1)
    slots = jnp.arange(shards * CAP, dtype=jnp.int32)
    table = within[:, :, :, None] == slots
    return table.reshape(groups, shards * rows, local_experts * shards * CAP)


def per_device(
    attn_out,
    residual,
    out_weight,
    norm_gain,
    router_weight,
    routes,
    gate_up,
    down_weight,
    final_gain,
    kv_pages,
    page_pick,
    destination,
):
    groups = lax.axis_size("dp")
    shards = lax.axis_size("tensor")
    rows, width = residual.shape
    local_experts = gate_up.shape[0]
    first = lax.axis_index("dp") * local_experts
    arrived = migrate(kv_pages, page_pick, destination)
    routes_all = lax.all_gather(routes, ("dp", "tensor"), axis=0, tiled=True)
    table = local_slots(routes_all, first, local_experts, groups, shards, rows)
    projected = lax.psum_scatter(
        jnp.dot(attn_out, out_weight, preferred_element_type=jnp.float32).astype(jnp.bfloat16),
        "tensor",
        scatter_dimension=0,
        tiled=True,
    ).astype(jnp.float32)
    mixed_sum = residual.astype(jnp.float32) + projected
    normed_in = rms_scale(mixed_sum, norm_gain).astype(jnp.bfloat16)
    tokens = lax.all_gather(normed_in, ("dp", "tensor"), axis=0, tiled=True)
    local_router = lax.dynamic_slice_in_dim(router_weight, first, local_experts, axis=1)
    logits = jnp.dot(tokens, local_router, preferred_element_type=jnp.float32)
    gates = jax.nn.sigmoid(logits).astype(jnp.bfloat16)
    tokens = tokens.reshape(groups, shards * rows, width)
    gates = jnp.repeat(
        gates.reshape(groups, shards * rows, local_experts), shards * CAP, axis=2
    )
    placement = table.astype(jnp.bfloat16)
    combine = jnp.where(table, gates, jnp.zeros((), jnp.bfloat16))
    slotted = jnp.einsum(
        "bts,btd->bsd", placement, tokens, preferred_element_type=jnp.float32
    ).astype(jnp.bfloat16)
    slotted = slotted.reshape(groups, local_experts, shards * CAP, width)
    paired = jnp.einsum(
        "becd,edgf->becgf", slotted, gate_up, preferred_element_type=jnp.float32
    )
    hidden = (jax.nn.silu(paired[..., 0, :]) * paired[..., 1, :]).astype(jnp.bfloat16)
    expert_out = jnp.einsum(
        "becf,efd->becd", hidden, down_weight, preferred_element_type=jnp.float32
    ).astype(jnp.bfloat16)
    expert_out = expert_out.reshape(groups, local_experts * shards * CAP, width)
    partial = jnp.einsum(
        "bts,bsd->btd", combine, expert_out, preferred_element_type=jnp.float32
    ).astype(jnp.bfloat16)
    moe_sum = lax.psum_scatter(
        partial.reshape(groups * shards * rows, width),
        ("dp", "tensor"),
        scatter_dimension=0,
        tiled=True,
    ).astype(jnp.float32)
    combined = mixed_sum + moe_sum
    new_residual = combined.astype(jnp.bfloat16)
    normed = rms_scale(combined, final_gain).astype(jnp.bfloat16)
    return (new_residual, normed, arrived)


def solution(mesh):
    in_specs = (
        P("dp", "tensor"),
        P(("dp", "tensor"), None),
        P("tensor", None),
        P(),
        P(),
        P(("dp", "tensor"), None),
        P("dp", None, None, "tensor"),
        P("dp", "tensor", None),
        P(),
        P("dp", None, "tensor", None),
        P("dp", None),
        P("dp", None),
    )
    out_specs = (
        P(("dp", "tensor"), None),
        P(("dp", "tensor"), None),
        P("dp", None, "tensor", None),
    )
    return jax.shard_map(
        per_device, mesh=mesh, in_specs=in_specs, out_specs=out_specs, check_vma=False
    )
```

```python
import jax
import jax.numpy as jnp
from jax import lax
from jax.experimental import pallas as pl
from jax.experimental.pallas import tpu as pltpu
from jax.sharding import PartitionSpec as P

CAP = 8


def rms_scale(values, gain_vec):
    mean_sq = jnp.mean(values * values, axis=-1, keepdims=True)
    return values * lax.rsqrt(mean_sq + 1e-06) * gain_vec


MESH = pl.DeviceIdType.MESH
EXTRA = 128


class Place:
    def __init__(self):
        group, shard = lax.axis_index("dp"), lax.axis_index("tensor")
        self.z, self.y = group // 2, group % 2
        self.x, self.c = shard // 2, shard % 2
        self.core_peer = (group, self.x * 2 + 1 - self.c)
        self.x_peer = (group, (1 - self.x) * 2 + self.c)
        self.y_peer = (self.z * 2 + 1 - self.y, shard)
        self.z_peers = [None] + [(((self.z + j) % 4) * 2 + self.y, shard) for j in (1, 2, 3)]

    def enter(self):
        barrier = pltpu.get_barrier_semaphore()
        peers = [self.core_peer, self.x_peer, self.y_peer] + self.z_peers[1:]
        for peer in peers:
            pl.semaphore_signal(barrier, inc=1, device_id=peer, device_id_type=MESH)
        pl.semaphore_wait(barrier, len(peers))


def sender(send_sems, recv_sems):
    used = []

    def send(source, target, peer):
        index = len(used)
        copy = pltpu.make_async_remote_copy(
            src_ref=source,
            dst_ref=target,
            send_sem=send_sems.at[index],
            recv_sem=recv_sems.at[index],
            device_id=peer,
            device_id_type=MESH,
        )
        copy.start()
        used.append(copy)
        return copy

    return send, used


def front_kernel(
    attn_ref, weight_ref, residual_ref, gain_ref, extra_ref, mixed_ref, all_ref,
    made, core_in, x_out, x_in, own, own_sem, send_sems, recv_sems,
):
    at = Place()
    z, y, x, c = at.z, at.y, at.x, at.c
    at.enter()
    send, used = sender(send_sems, recv_sems)
    rows, width = residual_ref.shape
    step = 512
    for start in range(0, width, step):
        part = jnp.dot(
            attn_ref[...], weight_ref[:, start : start + step], preferred_element_type=jnp.float32
        )
        for shard in range(4):
            made[shard, :, start : start + step] = part[
                shard * rows : (shard + 1) * rows
            ].astype(jnp.bfloat16)
    to_core_far = send(made.at[(1 - x) * 2 + 1 - c], core_in.at[0], at.core_peer)
    to_core_near = send(made.at[x * 2 + 1 - c], core_in.at[1], at.core_peer)
    to_core_far.wait_recv()
    x_out[...] = (
        made[(1 - x) * 2 + c].astype(jnp.float32) + core_in[0].astype(jnp.float32)
    ).astype(jnp.bfloat16)
    to_x = send(x_out, x_in, at.x_peer)
    to_core_near.wait_recv()
    mixed = (
        residual_ref[...].astype(jnp.float32)
        + made[x * 2 + c].astype(jnp.float32)
        + core_in[1].astype(jnp.float32)
    )
    to_x.wait_recv()
    mixed = mixed + x_in[...].astype(jnp.float32)
    mixed_ref[...] = mixed
    mean_sq = jnp.mean(mixed * mixed, axis=-1, keepdims=True)
    own[:, :width] = (mixed * lax.rsqrt(mean_sq + 1e-06) * gain_ref[...]).astype(jnp.bfloat16)
    own[:, width:] = extra_ref[...]

    half = width // 2
    columns = [pl.ds(0, half), pl.ds(half, half + EXTRA)]
    first_peer, second_peer = [at.y_peer, at.x_peer], [at.x_peer, at.y_peer]

    def block(h, zs, first_other, second_other):
        ys = first_other if h == 0 else second_other
        xs = second_other if h == 0 else first_other
        return all_ref.at[zs, 1 - y if ys else y, 1 - x if xs else x, c, :, columns[h]]

    def source(j):
        return (z + 4 - j) % 4

    z_copies, first_copies, second_copies, core_copies = {}, {}, {}, []
    for j in (1, 2, 3):
        for h in (0, 1):
            z_copies[h, j] = send(own.at[:, columns[h]], block(h, z, 0, 0), at.z_peers[j])
    keep = pltpu.make_async_copy(own, all_ref.at[z, y, x, c], own_sem)
    keep.start()
    for j in range(4):
        for h in (0, 1):
            mine = block(h, source(j), 0, 0)
            if j:
                z_copies[h, j].wait_recv()
            held = mine if j else own.at[:, columns[h]]
            first_copies[h, j] = send(held, mine, first_peer[h])
            second_copies[h, j, 0] = send(held, mine, second_peer[h])
            core_copies.append(send(held, mine, at.core_peer))
    for j in range(4):
        for h in (0, 1):
            first_copies[h, j].wait_recv()
            mine = block(h, source(j), 1, 0)
            second_copies[h, j, 1] = send(mine, mine, second_peer[h])
            core_copies.append(send(mine, mine, at.core_peer))
    for other in (0, 1):
        for j in range(4):
            for h in (0, 1):
                second_copies[h, j, other].wait_recv()
                mine = block(h, source(j), other, 1)
                core_copies.append(send(mine, mine, at.core_peer))
    for copy in core_copies:
        copy.wait_recv()
    for copy in used:
        copy.wait_send()
    keep.wait()


FRONT_COPIES = 3 + 2 * (3 + 4 + 8 + 16)


def front(attn_out, out_weight, residual, norm_gain, extra):
    rows, width = residual.shape
    vmem = pl.BlockSpec(memory_space=pltpu.VMEM)
    return pl.pallas_call(
        front_kernel,
        out_shape=(
            jax.ShapeDtypeStruct((rows, width), jnp.float32),
            jax.ShapeDtypeStruct((4, 2, 2, 2, rows, width + EXTRA), jnp.bfloat16),
        ),
        in_specs=[vmem] * 5,
        out_specs=(vmem, pl.BlockSpec(memory_space=pl.ANY)),
        scratch_shapes=[
            pltpu.VMEM((4, rows, width), jnp.bfloat16),
            pltpu.VMEM((2, rows, width), jnp.bfloat16),
            pltpu.VMEM((rows, width), jnp.bfloat16),
            pltpu.VMEM((rows, width), jnp.bfloat16),
            pltpu.VMEM((rows, width + EXTRA), jnp.bfloat16),
            pltpu.SemaphoreType.DMA,
            pltpu.SemaphoreType.DMA((FRONT_COPIES,)),
            pltpu.SemaphoreType.DMA((FRONT_COPIES,)),
        ],
        compiler_params=pltpu.CompilerParams(
            collective_id=0, has_side_effects=True, vmem_limit_bytes=40 << 20
        ),
        name="front",
    )(attn_out, out_weight, residual, norm_gain.reshape(1, width), extra)


def back_kernel(
    partial_ref, mixed_ref, gain_ref, new_ref, normed_ref,
    core_in, first_out, first_in, second_out, second_in, z_out, z_in, send_sems, recv_sems,
):
    at = Place()
    z, y, x, c = at.z, at.y, at.x, at.c
    at.enter()
    send, used = sender(send_sems, recv_sems)
    rows, width = mixed_ref.shape
    half = width // 2
    columns = [pl.ds(0, half), pl.ds(half, half)]
    first_peer, second_peer = [at.x_peer, at.y_peer], [at.y_peer, at.x_peer]
    order = (1, 2, 3, 0)

    def block(h, j, first_other, second_other, core):
        xs = first_other if h == 0 else second_other
        ys = second_other if h == 0 else first_other
        return (
            (z + j) % 4, 1 - y if ys else y, 1 - x if xs else x, core, slice(None), columns[h],
        )

    def wide(value):
        return value.astype(jnp.float32)

    core_copies, first_copies, second_copies, z_copies = {}, {}, {}, {}
    for first_other in (1, 0):
        for j in order:
            for h in (0, 1):
                for second_other in (1, 0):
                    slot = (h, first_other, j, second_other)
                    core_copies[slot] = send(
                        partial_ref.at[block(h, j, first_other, second_other, 1 - c)],
                        core_in.at[slot],
                        at.core_peer,
                    )
    for j in order:
        for h in (0, 1):
            for second_other in (1, 0):
                core_copies[h, 1, j, second_other].wait_recv()
                first_out[h, j, second_other] = (
                    wide(partial_ref[block(h, j, 1, second_other, c)])
                    + wide(core_in[h, 1, j, second_other])
                ).astype(jnp.bfloat16)
                slot = (h, j, second_other)
                first_copies[slot] = send(first_out.at[slot], first_in.at[slot], first_peer[h])

    def gathered(h, j, second_other):
        core_copies[h, 0, j, second_other].wait_recv()
        first_copies[h, j, second_other].wait_recv()
        return (
            wide(partial_ref[block(h, j, 0, second_other, c)])
            + wide(core_in[h, 0, j, second_other])
            + wide(first_in[h, j, second_other])
        )

    for j in order:
        for h in (0, 1):
            second_out[h, j] = gathered(h, j, 1).astype(jnp.bfloat16)
            second_copies[h, j] = send(second_out.at[h, j], second_in.at[h, j], second_peer[h])
    for j in order:
        for h in (0, 1):
            total = gathered(h, j, 0)
            second_copies[h, j].wait_recv()
            total = total + wide(second_in[h, j])
            if j:
                z_out[h, j - 1] = total.astype(jnp.bfloat16)
                z_copies[h, j] = send(z_out.at[h, j - 1], z_in.at[h, j - 1], at.z_peers[j])
            else:
                mixed_half = mixed_ref[:, columns[h]] + total
                for k in (1, 2, 3):
                    z_copies[h, k].wait_recv()
                    mixed_half = mixed_half + wide(z_in[h, k - 1])
                if h == 0:
                    left = mixed_half
    right = mixed_half
    total_sq = jnp.sum(left * left, axis=-1, keepdims=True) + jnp.sum(
        right * right, axis=-1, keepdims=True
    )
    scale = lax.rsqrt(total_sq / width + 1e-06)
    for h, value in enumerate((left, right)):
        new_ref[:, columns[h]] = value.astype(jnp.bfloat16)
        normed_ref[:, columns[h]] = (value * scale * gain_ref[:, columns[h]]).astype(jnp.bfloat16)
    for copy in used:
        copy.wait_send()


BACK_COPIES = 2 * (16 + 8 + 4 + 3)


def back(partial, mixed, final_gain):
    rows, width = mixed.shape
    half = width // 2
    vmem = pl.BlockSpec(memory_space=pltpu.VMEM)
    blocks = lambda *lead: pltpu.VMEM(lead + (rows, half), jnp.bfloat16)
    return pl.pallas_call(
        back_kernel,
        out_shape=(jax.ShapeDtypeStruct((rows, width), jnp.bfloat16),) * 2,
        in_specs=[vmem] * 3,
        out_specs=(vmem, vmem),
        scratch_shapes=[
            blocks(2, 2, 4, 2),
            blocks(2, 4, 2),
            blocks(2, 4, 2),
            blocks(2, 4),
            blocks(2, 4),
            blocks(2, 3),
            blocks(2, 3),
            pltpu.SemaphoreType.DMA((BACK_COPIES,)),
            pltpu.SemaphoreType.DMA((BACK_COPIES,)),
        ],
        compiler_params=pltpu.CompilerParams(
            collective_id=1, has_side_effects=True, vmem_limit_bytes=40 << 20
        ),
        name="back",
    )(partial, mixed, final_gain.reshape(1, width))


def migrate(kv_pages, page_pick, destination):
    groups = lax.axis_size("dp")
    chosen_pages = kv_pages[page_pick[0]]
    owners = jnp.arange(groups, dtype=jnp.int32)[:, None] == destination[0][None, :]
    outgoing = jnp.where(
        owners[:, :, None, None, None], chosen_pages[None], jnp.zeros((), kv_pages.dtype)
    )
    incoming = lax.all_to_all(outgoing, "dp", split_axis=0, concat_axis=0, tiled=True)
    return jnp.sum(incoming, axis=0)


def local_slots(routes_all, first, local_experts, groups, shards, rows):
    hits = jnp.any(
        routes_all[:, :, None] == first + jnp.arange(local_experts, dtype=jnp.int32), axis=1
    )
    hits = hits.reshape(groups, shards * rows, local_experts)
    token = jnp.arange(shards * rows, dtype=jnp.int32)
    before = (token[:, None] > token[None, :]) & (
        token[:, None] // rows == token[None, :] // rows
    )
    rank = jnp.einsum(
        "ut,bte->bue",
        before.astype(jnp.bfloat16),
        hits.astype(jnp.bfloat16),
        preferred_element_type=jnp.float32,
    ).astype(jnp.int32)
    within = (token // rows * CAP)[None, :, None] + rank
    within = jnp.where(hits, within, -1)
    slots = jnp.arange(shards * CAP, dtype=jnp.int32)
    table = within[:, :, :, None] == slots
    return table.reshape(groups, shards * rows, local_experts * shards * CAP)


def per_device(
    attn_out,
    residual,
    out_weight,
    norm_gain,
    router_weight,
    routes,
    gate_up,
    down_weight,
    final_gain,
    kv_pages,
    page_pick,
    destination,
):
    groups = lax.axis_size("dp")
    shards = lax.axis_size("tensor")
    rows, width = residual.shape
    local_experts = gate_up.shape[0]
    first = lax.axis_index("dp") * local_experts
    grid = groups == 8 and shards == 4
    if grid:
        top_count = routes.shape[1]
        extra = jnp.concatenate(
            [routes, jnp.broadcast_to(destination, (rows, destination.shape[1]))], axis=1
        ).astype(jnp.bfloat16)
        extra = jnp.pad(extra, ((0, 0), (0, EXTRA - extra.shape[1])))
        pages_all = lax.all_gather(kv_pages[page_pick[0]], "dp", axis=0)
        mixed_sum, everything = front(attn_out, out_weight, residual, norm_gain, extra)
        everything = everything.reshape(groups, shards * rows, width + EXTRA)
        tokens = everything[:, :, :width].reshape(-1, width)
        tail = everything[:, :, width:].astype(jnp.int32)
        routes_all = tail[:, :, :top_count].reshape(-1, top_count)
        owners = tail[:, 0, top_count : top_count + destination.shape[1]]
        chosen = (owners == lax.axis_index("dp"))[:, :, None, None, None]
        arrived = jnp.sum(jnp.where(chosen, pages_all, jnp.zeros((), kv_pages.dtype)), axis=0)
    else:
        arrived = migrate(kv_pages, page_pick, destination)
        routes_all = lax.all_gather(routes, ("dp", "tensor"), axis=0, tiled=True)
        projected = lax.psum_scatter(
            jnp.dot(attn_out, out_weight, preferred_element_type=jnp.float32).astype(
                jnp.bfloat16
            ),
            "tensor",
            scatter_dimension=0,
            tiled=True,
        ).astype(jnp.float32)
        mixed_sum = residual.astype(jnp.float32) + projected
        normed_in = rms_scale(mixed_sum, norm_gain).astype(jnp.bfloat16)
        tokens = lax.all_gather(normed_in, ("dp", "tensor"), axis=0, tiled=True)
    table = local_slots(routes_all, first, local_experts, groups, shards, rows)
    local_router = lax.dynamic_slice_in_dim(router_weight, first, local_experts, axis=1)
    logits = jnp.dot(tokens, local_router, preferred_element_type=jnp.float32)
    gates = jax.nn.sigmoid(logits).astype(jnp.bfloat16)
    tokens = tokens.reshape(groups, shards * rows, width)
    gates = jnp.repeat(
        gates.reshape(groups, shards * rows, local_experts), shards * CAP, axis=2
    )
    placement = table.astype(jnp.bfloat16)
    combine = jnp.where(table, gates, jnp.zeros((), jnp.bfloat16))
    slotted = jnp.einsum(
        "bts,btd->bsd", placement, tokens, preferred_element_type=jnp.float32
    ).astype(jnp.bfloat16)
    slotted = slotted.reshape(groups, local_experts, shards * CAP, width)
    paired = jnp.einsum(
        "becd,edgf->becgf", slotted, gate_up, preferred_element_type=jnp.float32
    )
    hidden = (jax.nn.silu(paired[..., 0, :]) * paired[..., 1, :]).astype(jnp.bfloat16)
    expert_out = jnp.einsum(
        "becf,efd->becd", hidden, down_weight, preferred_element_type=jnp.float32
    ).astype(jnp.bfloat16)
    expert_out = expert_out.reshape(groups, local_experts * shards * CAP, width)
    partial = jnp.einsum(
        "bts,bsd->btd", combine, expert_out, preferred_element_type=jnp.float32
    ).astype(jnp.bfloat16)
    if grid:
        new_residual, normed = back(
            partial.reshape(4, 2, 2, 2, rows, width), mixed_sum, final_gain
        )
        return (new_residual, normed, arrived)
    moe_sum = lax.psum_scatter(
        partial.reshape(groups * shards * rows, width),
        ("dp", "tensor"),
        scatter_dimension=0,
        tiled=True,
    ).astype(jnp.float32)
    combined = mixed_sum + moe_sum
    new_residual = combined.astype(jnp.bfloat16)
    normed = rms_scale(combined, final_gain).astype(jnp.bfloat16)
    return (new_residual, normed, arrived)


def solution(mesh):
    in_specs = (
        P("dp", "tensor"),
        P(("dp", "tensor"), None),
        P("tensor", None),
        P(),
        P(),
        P(("dp", "tensor"), None),
        P("dp", None, None, "tensor"),
        P("dp", "tensor", None),
        P(),
        P("dp", None, "tensor", None),
        P("dp", None),
        P("dp", None),
    )
    out_specs = (
        P(("dp", "tensor"), None),
        P(("dp", "tensor"), None),
        P("dp", None, "tensor", None),
    )
    return jax.shard_map(
        per_device, mesh=mesh, in_specs=in_specs, out_specs=out_specs, check_vma=False
    )
```

```python
import jax
import jax.numpy as jnp
from jax import lax
from jax.experimental import pallas as pl
from jax.experimental.pallas import tpu as pltpu
from jax.sharding import PartitionSpec as P

CAP = 8


def rms_scale(values, gain_vec):
    mean_sq = jnp.mean(values * values, axis=-1, keepdims=True)
    return values * lax.rsqrt(mean_sq + 1e-06) * gain_vec


MESH = pl.DeviceIdType.MESH
EXTRA = 128


class Place:
    def __init__(self):
        group, shard = lax.axis_index("dp"), lax.axis_index("tensor")
        self.z, self.y = group // 2, group % 2
        self.x, self.c = shard // 2, shard % 2
        self.core_peer = (group, self.x * 2 + 1 - self.c)
        self.x_peer = (group, (1 - self.x) * 2 + self.c)
        self.y_peer = (self.z * 2 + 1 - self.y, shard)
        self.z_peers = [None] + [(((self.z + j) % 4) * 2 + self.y, shard) for j in (1, 2, 3)]

    def enter(self):
        barrier = pltpu.get_barrier_semaphore()
        peers = [self.core_peer, self.x_peer, self.y_peer] + self.z_peers[1:]
        for peer in peers:
            pl.semaphore_signal(barrier, inc=1, device_id=peer, device_id_type=MESH)
        pl.semaphore_wait(barrier, len(peers))


def sender(send_sems, recv_sems):
    used = []

    def send(source, target, peer):
        index = len(used)
        copy = pltpu.make_async_remote_copy(
            src_ref=source,
            dst_ref=target,
            send_sem=send_sems.at[index],
            recv_sem=recv_sems.at[index],
            device_id=peer,
            device_id_type=MESH,
        )
        copy.start()
        used.append(copy)
        return copy

    return send, used


def front_kernel(
    attn_ref, weight_ref, residual_ref, gain_ref, extra_ref, mixed_ref, all_ref,
    made, core_in, x_out, x_in, own, own_sem, send_sems, recv_sems,
):
    at = Place()
    z, y, x, c = at.z, at.y, at.x, at.c
    at.enter()
    send, used = sender(send_sems, recv_sems)
    rows, width = residual_ref.shape
    step = 512
    for start in range(0, width, step):
        part = jnp.dot(
            attn_ref[...], weight_ref[:, start : start + step], preferred_element_type=jnp.float32
        )
        for shard in range(4):
            made[shard, :, start : start + step] = part[
                shard * rows : (shard + 1) * rows
            ].astype(jnp.bfloat16)
    to_core_far = send(made.at[(1 - x) * 2 + 1 - c], core_in.at[0], at.core_peer)
    to_core_near = send(made.at[x * 2 + 1 - c], core_in.at[1], at.core_peer)
    to_core_far.wait_recv()
    x_out[...] = (
        made[(1 - x) * 2 + c].astype(jnp.float32) + core_in[0].astype(jnp.float32)
    ).astype(jnp.bfloat16)
    to_x = send(x_out, x_in, at.x_peer)
    to_core_near.wait_recv()
    mixed = (
        residual_ref[...].astype(jnp.float32)
        + made[x * 2 + c].astype(jnp.float32)
        + core_in[1].astype(jnp.float32)
    )
    to_x.wait_recv()
    mixed = mixed + x_in[...].astype(jnp.float32)
    mixed_ref[...] = mixed
    mean_sq = jnp.mean(mixed * mixed, axis=-1, keepdims=True)
    own[:, :width] = (mixed * lax.rsqrt(mean_sq + 1e-06) * gain_ref[...]).astype(jnp.bfloat16)
    own[:, width:] = extra_ref[...]

    half = width // 2
    columns = [pl.ds(0, half), pl.ds(half, half + EXTRA)]
    first_peer, second_peer = [at.y_peer, at.x_peer], [at.x_peer, at.y_peer]

    def block(h, zs, first_other, second_other):
        ys = first_other if h == 0 else second_other
        xs = second_other if h == 0 else first_other
        return all_ref.at[zs, 1 - y if ys else y, 1 - x if xs else x, c, :, columns[h]]

    def source(j):
        return (z + 4 - j) % 4

    z_copies, first_copies, second_copies, core_copies = {}, {}, {}, []
    for j in (1, 2, 3):
        for h in (0, 1):
            z_copies[h, j] = send(own.at[:, columns[h]], block(h, z, 0, 0), at.z_peers[j])
    keep = pltpu.make_async_copy(own, all_ref.at[z, y, x, c], own_sem)
    keep.start()
    for j in range(4):
        for h in (0, 1):
            mine = block(h, source(j), 0, 0)
            if j:
                z_copies[h, j].wait_recv()
            held = mine if j else own.at[:, columns[h]]
            first_copies[h, j] = send(held, mine, first_peer[h])
            second_copies[h, j, 0] = send(held, mine, second_peer[h])
            core_copies.append(send(held, mine, at.core_peer))
    for j in range(4):
        for h in (0, 1):
            first_copies[h, j].wait_recv()
            mine = block(h, source(j), 1, 0)
            second_copies[h, j, 1] = send(mine, mine, second_peer[h])
            core_copies.append(send(mine, mine, at.core_peer))
    for other in (0, 1):
        for j in range(4):
            for h in (0, 1):
                second_copies[h, j, other].wait_recv()
                mine = block(h, source(j), other, 1)
                core_copies.append(send(mine, mine, at.core_peer))
    for copy in core_copies:
        copy.wait_recv()
    for copy in used:
        copy.wait_send()
    keep.wait()


FRONT_COPIES = 3 + 2 * (3 + 4 + 8 + 16)


def front(attn_out, out_weight, residual, norm_gain, extra):
    rows, width = residual.shape
    vmem = pl.BlockSpec(memory_space=pltpu.VMEM)
    return pl.pallas_call(
        front_kernel,
        out_shape=(
            jax.ShapeDtypeStruct((rows, width), jnp.float32),
            jax.ShapeDtypeStruct((4, 2, 2, 2, rows, width + EXTRA), jnp.bfloat16),
        ),
        in_specs=[vmem] * 5,
        out_specs=(vmem, pl.BlockSpec(memory_space=pl.ANY)),
        scratch_shapes=[
            pltpu.VMEM((4, rows, width), jnp.bfloat16),
            pltpu.VMEM((2, rows, width), jnp.bfloat16),
            pltpu.VMEM((rows, width), jnp.bfloat16),
            pltpu.VMEM((rows, width), jnp.bfloat16),
            pltpu.VMEM((rows, width + EXTRA), jnp.bfloat16),
            pltpu.SemaphoreType.DMA,
            pltpu.SemaphoreType.DMA((FRONT_COPIES,)),
            pltpu.SemaphoreType.DMA((FRONT_COPIES,)),
        ],
        compiler_params=pltpu.CompilerParams(
            collective_id=0, has_side_effects=True, vmem_limit_bytes=40 << 20
        ),
        name="front",
    )(attn_out, out_weight, residual, norm_gain.reshape(1, width), extra)


def back_kernel(
    partial_ref, mixed_ref, gain_ref, pages_ref, chosen_ref, new_ref, normed_ref, arrived_ref,
    pages_in, core_in, first_out, first_in, second_out, second_in, z_out, z_in, send_sems, recv_sems,
):
    at = Place()
    z, y, x, c = at.z, at.y, at.x, at.c
    at.enter()
    send, used = sender(send_sems, recv_sems)
    rows, width = mixed_ref.shape
    half = width // 2
    columns = [pl.ds(0, half), pl.ds(half, half)]
    first_peer, second_peer = [at.x_peer, at.y_peer], [at.y_peer, at.x_peer]
    order = (1, 2, 3, 0)

    def block(h, j, first_other, second_other, core):
        xs = first_other if h == 0 else second_other
        ys = second_other if h == 0 else first_other
        return (
            (z + j) % 4, 1 - y if ys else y, 1 - x if xs else x, core, slice(None), columns[h],
        )

    def wide(value):
        return value.astype(jnp.float32)

    core_copies, first_copies, second_copies, z_copies = {}, {}, {}, {}
    page_z = [
        send(pages_ref, pages_in.at[j, 0], at.z_peers[j]) if j else None for j in range(4)
    ]
    for first_other in (1, 0):
        for j in order:
            for h in (0, 1):
                for second_other in (1, 0):
                    slot = (h, first_other, j, second_other)
                    core_copies[slot] = send(
                        partial_ref.at[block(h, j, first_other, second_other, 1 - c)],
                        core_in.at[slot],
                        at.core_peer,
                    )
    for j in order:
        for h in (0, 1):
            for second_other in (1, 0):
                core_copies[h, 1, j, second_other].wait_recv()
                first_out[h, j, second_other] = (
                    wide(partial_ref[block(h, j, 1, second_other, c)])
                    + wide(core_in[h, 1, j, second_other])
                ).astype(jnp.bfloat16)
                slot = (h, j, second_other)
                first_copies[slot] = send(first_out.at[slot], first_in.at[slot], first_peer[h])

    def gathered(h, j, second_other):
        core_copies[h, 0, j, second_other].wait_recv()
        first_copies[h, j, second_other].wait_recv()
        return (
            wide(partial_ref[block(h, j, 0, second_other, c)])
            + wide(core_in[h, 0, j, second_other])
            + wide(first_in[h, j, second_other])
        )

    for j in order:
        for h in (0, 1):
            second_out[h, j] = gathered(h, j, 1).astype(jnp.bfloat16)
            second_copies[h, j] = send(second_out.at[h, j], second_in.at[h, j], second_peer[h])
    page_y = []
    for j in range(4):
        if j:
            page_z[j].wait_recv()
        held = pages_in.at[j, 0] if j else pages_ref
        page_y.append(send(held, pages_in.at[j, 1], at.y_peer))
    for j in order:
        for h in (0, 1):
            total = gathered(h, j, 0)
            second_copies[h, j].wait_recv()
            total = total + wide(second_in[h, j])
            if j:
                z_out[h, j - 1] = total.astype(jnp.bfloat16)
                z_copies[h, j] = send(z_out.at[h, j - 1], z_in.at[h, j - 1], at.z_peers[j])
            else:
                mixed_half = mixed_ref[:, columns[h]] + total
                for k in (1, 2, 3):
                    z_copies[h, k].wait_recv()
                    mixed_half = mixed_half + wide(z_in[h, k - 1])
                if h == 0:
                    left = mixed_half
    right = mixed_half
    total_sq = jnp.sum(left * left, axis=-1, keepdims=True) + jnp.sum(
        right * right, axis=-1, keepdims=True
    )
    scale = lax.rsqrt(total_sq / width + 1e-06)
    for h, value in enumerate((left, right)):
        new_ref[:, columns[h]] = value.astype(jnp.bfloat16)
        normed_ref[:, columns[h]] = (value * scale * gain_ref[:, columns[h]]).astype(jnp.bfloat16)
    for copy in page_y:
        copy.wait_recv()
    for slot in range(pages_ref.shape[0]):
        found = jnp.zeros(pages_ref.shape[1:], jnp.float32)
        for j in range(4):
            for other in (0, 1):
                held = pages_in[j, other, slot] if j or other else pages_ref[slot]
                found = found + jnp.where(chosen_ref[slot, j, other] > 0, wide(held), 0.0)
        arrived_ref[slot] = found.astype(jnp.bfloat16)
    for copy in used:
        copy.wait_send()


BACK_COPIES = 2 * (16 + 8 + 4 + 3) + 7


def back(partial, mixed, final_gain, pages, chosen):
    rows, width = mixed.shape
    half = width // 2
    vmem = pl.BlockSpec(memory_space=pltpu.VMEM)
    blocks = lambda *lead: pltpu.VMEM(lead + (rows, half), jnp.bfloat16)
    return pl.pallas_call(
        back_kernel,
        out_shape=(jax.ShapeDtypeStruct((rows, width), jnp.bfloat16),) * 2
        + (jax.ShapeDtypeStruct(pages.shape, jnp.bfloat16),),
        in_specs=[vmem] * 5,
        out_specs=(vmem,) * 3,
        scratch_shapes=[
            pltpu.VMEM((4, 2) + pages.shape, jnp.bfloat16),
            blocks(2, 2, 4, 2),
            blocks(2, 4, 2),
            blocks(2, 4, 2),
            blocks(2, 4),
            blocks(2, 4),
            blocks(2, 3),
            blocks(2, 3),
            pltpu.SemaphoreType.DMA((BACK_COPIES,)),
            pltpu.SemaphoreType.DMA((BACK_COPIES,)),
        ],
        compiler_params=pltpu.CompilerParams(
            collective_id=1, has_side_effects=True, vmem_limit_bytes=40 << 20
        ),
        name="back",
    )(partial, mixed, final_gain.reshape(1, width), pages, chosen)

def dispatch_kernel(rows, top_count, all_ref, router_ref, named_ref, slots_ref, combine_ref):
    width = router_ref.shape[0]
    block = all_ref.shape[1]
    span = router_ref.shape[1]
    lanes = slots_ref.shape[2]
    tokens = all_ref[0, :, :width]
    tail = all_ref[0, :, width:].astype(jnp.float32)
    named = named_ref[...]
    hits = jnp.zeros((block, span), jnp.float32)
    for k in range(top_count):
        hits = hits + jnp.where(tail[:, k : k + 1] == named, 1.0, 0.0)
    later = lax.broadcasted_iota(jnp.int32, (block, block), 0)
    sooner = lax.broadcasted_iota(jnp.int32, (block, block), 1)
    before = (later > sooner) & (later // rows == sooner // rows)
    rank = jnp.dot(
        jnp.where(before, 1.0, 0.0).astype(jnp.bfloat16),
        hits.astype(jnp.bfloat16),
        preferred_element_type=jnp.float32,
    )
    owner = lax.broadcasted_iota(jnp.int32, (block, span), 0) // rows
    slot = lax.broadcasted_iota(jnp.int32, (block, span), 1) % lanes
    wanted = (slot - owner * CAP).astype(jnp.float32)
    table = jnp.where((hits > 0) & (rank == wanted), 1.0, 0.0)
    logits = jnp.dot(tokens, router_ref[...], preferred_element_type=jnp.float32)
    combine_ref[0] = (table * jax.nn.sigmoid(logits)).astype(jnp.bfloat16)
    placed = lax.dot_general(
        table.astype(jnp.bfloat16),
        tokens,
        (((0,), (0,)), ((), ())),
        preferred_element_type=jnp.float32,
    ).astype(jnp.bfloat16)
    for e in range(slots_ref.shape[0]):
        slots_ref[e, 0] = placed[e * lanes : (e + 1) * lanes]


def dispatch(everything, router_slots, named, local_experts, rows, top_count):
    groups, block, wide = everything.shape
    width, span = router_slots.shape
    lanes = span // local_experts
    return pl.pallas_call(
        lambda *refs: dispatch_kernel(rows, top_count, *refs),
        grid=(groups,),
        out_shape=(
            jax.ShapeDtypeStruct((local_experts, groups, lanes, width), jnp.bfloat16),
            jax.ShapeDtypeStruct((groups, block, span), jnp.bfloat16),
        ),
        in_specs=[
            pl.BlockSpec((1, block, wide), lambda b: (b, 0, 0)),
            pl.BlockSpec((width, span), lambda b: (0, 0)),
            pl.BlockSpec((1, span), lambda b: (0, 0)),
        ],
        out_specs=(
            pl.BlockSpec((local_experts, 1, lanes, width), lambda b: (0, b, 0, 0)),
            pl.BlockSpec((1, block, span), lambda b: (b, 0, 0)),
        ),
        compiler_params=pltpu.CompilerParams(vmem_limit_bytes=40 << 20),
        name="dispatch",
    )(everything, router_slots, named)


def finish_kernel(experts, groups, paired_ref, down_ref, combine_ref, out_ref, held):
    step = pl.program_id(0)
    lanes = held.shape[1] // experts

    @pl.when(step < experts)
    def _():
        gate, up = paired_ref[0, 0], paired_ref[0, 1]
        hidden = (gate / (1.0 + jnp.exp(-gate)) * up).astype(jnp.bfloat16)
        made = jnp.dot(hidden, down_ref[0], preferred_element_type=jnp.float32)
        spot = pl.ds(pl.multiple_of(step * lanes, lanes), lanes)
        for b in range(groups):
            held[b, spot, :] = made[b * lanes : (b + 1) * lanes].astype(jnp.bfloat16)

    @pl.when(step >= experts)
    def _():
        out_ref[0] = jnp.dot(
            combine_ref[0], held[step - experts], preferred_element_type=jnp.float32
        ).astype(jnp.bfloat16)


def finish(paired, down_weight, combine):
    experts, _, slots, units = paired.shape
    groups, block, span = combine.shape
    width = down_weight.shape[2]
    expert = lambda i: jnp.minimum(i, experts - 1)
    group = lambda i: jnp.maximum(i - experts, 0)
    return pl.pallas_call(
        lambda *refs: finish_kernel(experts, groups, *refs),
        grid=(experts + groups,),
        out_shape=jax.ShapeDtypeStruct((groups, block, width), jnp.bfloat16),
        in_specs=[
            pl.BlockSpec((1, 2, slots, units), lambda i: (expert(i), 0, 0, 0)),
            pl.BlockSpec((1, units, width), lambda i: (expert(i), 0, 0)),
            pl.BlockSpec((1, block, span), lambda i: (group(i), 0, 0)),
        ],
        out_specs=pl.BlockSpec((1, block, width), lambda i: (group(i), 0, 0)),
        scratch_shapes=[pltpu.VMEM((groups, span, width), jnp.bfloat16)],
        compiler_params=pltpu.CompilerParams(vmem_limit_bytes=40 << 20),
        name="finish",
    )(paired, down_weight, combine)


def migrate(kv_pages, page_pick, destination):
    groups = lax.axis_size("dp")
    chosen_pages = kv_pages[page_pick[0]]
    owners = jnp.arange(groups, dtype=jnp.int32)[:, None] == destination[0][None, :]
    outgoing = jnp.where(
        owners[:, :, None, None, None], chosen_pages[None], jnp.zeros((), kv_pages.dtype)
    )
    incoming = lax.all_to_all(outgoing, "dp", split_axis=0, concat_axis=0, tiled=True)
    return jnp.sum(incoming, axis=0)


def local_slots(routes_all, first, local_experts, groups, shards, rows):
    hits = jnp.any(
        routes_all[:, :, None] == first + jnp.arange(local_experts, dtype=jnp.int32), axis=1
    )
    hits = hits.reshape(groups, shards * rows, local_experts)
    token = jnp.arange(shards * rows, dtype=jnp.int32)
    before = (token[:, None] > token[None, :]) & (
        token[:, None] // rows == token[None, :] // rows
    )
    rank = jnp.einsum(
        "ut,bte->bue",
        before.astype(jnp.bfloat16),
        hits.astype(jnp.bfloat16),
        preferred_element_type=jnp.float32,
    ).astype(jnp.int32)
    within = (token // rows * CAP)[None, :, None] + rank
    within = jnp.where(hits, within, -1)
    slots = jnp.arange(shards * CAP, dtype=jnp.int32)
    table = within[:, :, :, None] == slots
    return table.reshape(groups, shards * rows, local_experts * shards * CAP)


def per_device(
    attn_out,
    residual,
    out_weight,
    norm_gain,
    router_weight,
    routes,
    gate_up,
    down_weight,
    final_gain,
    kv_pages,
    page_pick,
    destination,
):
    groups = lax.axis_size("dp")
    shards = lax.axis_size("tensor")
    rows, width = residual.shape
    local_experts = gate_up.shape[0]
    first = lax.axis_index("dp") * local_experts
    grid = groups == 8 and shards == 4
    if grid:
        top_count = routes.shape[1]
        extra = jnp.concatenate(
            [routes, jnp.broadcast_to(destination, (rows, destination.shape[1]))], axis=1
        ).astype(jnp.bfloat16)
        extra = jnp.pad(extra, ((0, 0), (0, EXTRA - extra.shape[1])))
        pages = kv_pages[page_pick[0]]
        moved = pages.reshape(pages.shape[0], pages.shape[1], -1)
        local_router = lax.dynamic_slice_in_dim(router_weight, first, local_experts, axis=1)
        router_slots = jnp.repeat(local_router, shards * CAP, axis=1)
        named = first + jnp.arange(local_experts * shards * CAP) // (shards * CAP)
        mixed_sum, everything = front(attn_out, out_weight, residual, norm_gain, extra)
        owners = everything[:, 0, 0, 0, 0, width + top_count : width + top_count + 2]
        owners_y = everything[:, 1, 0, 0, 0, width + top_count : width + top_count + 2]
        owners = jnp.stack([owners, owners_y], axis=1).astype(jnp.int32)
        chosen = owners == lax.axis_index("dp")
        depth, side = lax.axis_index("dp") // 2, lax.axis_index("dp") % 2
        chosen = chosen[(depth + 4 - jnp.arange(4)) % 4][:, (side + jnp.arange(2)) % 2]
        chosen = chosen.transpose(2, 0, 1).astype(jnp.float32)
        chosen = jnp.broadcast_to(chosen[..., None, None], chosen.shape + (1, moved.shape[2]))
        everything = everything.reshape(groups, shards * rows, width + EXTRA)
        slotted, combine = dispatch(
            everything,
            router_slots,
            named.astype(jnp.float32).reshape(1, -1),
            local_experts,
            rows,
            top_count,
        )
        paired = jnp.einsum(
            "emd,edgf->egmf",
            slotted.reshape(local_experts, -1, width),
            gate_up,
            preferred_element_type=jnp.float32,
        )
        partial = finish(paired, down_weight, combine)
        new_residual, normed, arrived = back(
            partial.reshape(4, 2, 2, 2, rows, width), mixed_sum, final_gain, moved, chosen
        )
        return (new_residual, normed, arrived.reshape(pages.shape))
    else:
        arrived = migrate(kv_pages, page_pick, destination)
        routes_all = lax.all_gather(routes, ("dp", "tensor"), axis=0, tiled=True)
        projected = lax.psum_scatter(
            jnp.dot(attn_out, out_weight, preferred_element_type=jnp.float32).astype(
                jnp.bfloat16
            ),
            "tensor",
            scatter_dimension=0,
            tiled=True,
        ).astype(jnp.float32)
        mixed_sum = residual.astype(jnp.float32) + projected
        normed_in = rms_scale(mixed_sum, norm_gain).astype(jnp.bfloat16)
        tokens = lax.all_gather(normed_in, ("dp", "tensor"), axis=0, tiled=True)
    table = local_slots(routes_all, first, local_experts, groups, shards, rows)
    local_router = lax.dynamic_slice_in_dim(router_weight, first, local_experts, axis=1)
    logits = jnp.dot(tokens, local_router, preferred_element_type=jnp.float32)
    gates = jax.nn.sigmoid(logits).astype(jnp.bfloat16)
    tokens = tokens.reshape(groups, shards * rows, width)
    gates = jnp.repeat(
        gates.reshape(groups, shards * rows, local_experts), shards * CAP, axis=2
    )
    placement = table.astype(jnp.bfloat16)
    combine = jnp.where(table, gates, jnp.zeros((), jnp.bfloat16))
    slotted = jnp.einsum(
        "bts,btd->bsd", placement, tokens, preferred_element_type=jnp.float32
    ).astype(jnp.bfloat16)
    slotted = slotted.reshape(groups, local_experts, shards * CAP, width)
    paired = jnp.einsum(
        "becd,edgf->becgf", slotted, gate_up, preferred_element_type=jnp.float32
    )
    hidden = (jax.nn.silu(paired[..., 0, :]) * paired[..., 1, :]).astype(jnp.bfloat16)
    expert_out = jnp.einsum(
        "becf,efd->becd", hidden, down_weight, preferred_element_type=jnp.float32
    ).astype(jnp.bfloat16)
    expert_out = expert_out.reshape(groups, local_experts * shards * CAP, width)
    partial = jnp.einsum(
        "bts,bsd->btd", combine, expert_out, preferred_element_type=jnp.float32
    ).astype(jnp.bfloat16)
    moe_sum = lax.psum_scatter(
        partial.reshape(groups * shards * rows, width),
        ("dp", "tensor"),
        scatter_dimension=0,
        tiled=True,
    ).astype(jnp.float32)
    combined = mixed_sum + moe_sum
    new_residual = combined.astype(jnp.bfloat16)
    normed = rms_scale(combined, final_gain).astype(jnp.bfloat16)
    return (new_residual, normed, arrived)


def solution(mesh):
    in_specs = (
        P("dp", "tensor"),
        P(("dp", "tensor"), None),
        P("tensor", None),
        P(),
        P(),
        P(("dp", "tensor"), None),
        P("dp", None, None, "tensor"),
        P("dp", "tensor", None),
        P(),
        P("dp", None, "tensor", None),
        P("dp", None),
        P("dp", None),
    )
    out_specs = (
        P(("dp", "tensor"), None),
        P(("dp", "tensor"), None),
        P("dp", None, "tensor", None),
    )
    return jax.shard_map(
        per_device, mesh=mesh, in_specs=in_specs, out_specs=out_specs, check_vma=False
    )
```

```python
import jax
import jax.numpy as jnp
from jax import lax
from jax.experimental import pallas as pl
from jax.experimental.pallas import tpu as pltpu
from jax.sharding import PartitionSpec as P

CAP = 8


def rms_scale(values, gain_vec):
    mean_sq = jnp.mean(values * values, axis=-1, keepdims=True)
    return values * lax.rsqrt(mean_sq + 1e-06) * gain_vec


MESH = pl.DeviceIdType.MESH
EXTRA = 128


class Place:
    def __init__(self):
        group, shard = lax.axis_index("dp"), lax.axis_index("tensor")
        self.z, self.y = group // 2, group % 2
        self.x, self.c = shard // 2, shard % 2
        self.core_peer = (group, self.x * 2 + 1 - self.c)
        self.x_peer = (group, (1 - self.x) * 2 + self.c)
        self.y_peer = (self.z * 2 + 1 - self.y, shard)
        self.z_peers = [None] + [(((self.z + j) % 4) * 2 + self.y, shard) for j in (1, 2, 3)]

    def enter(self):
        barrier = pltpu.get_barrier_semaphore()
        peers = [self.core_peer, self.x_peer, self.y_peer] + self.z_peers[1:]
        for peer in peers:
            pl.semaphore_signal(barrier, inc=1, device_id=peer, device_id_type=MESH)
        pl.semaphore_wait(barrier, len(peers))


def sender(send_sems, recv_sems):
    used = []

    def send(source, target, peer):
        index = len(used)
        copy = pltpu.make_async_remote_copy(
            src_ref=source,
            dst_ref=target,
            send_sem=send_sems.at[index],
            recv_sem=recv_sems.at[index],
            device_id=peer,
            device_id_type=MESH,
        )
        copy.start()
        used.append(copy)
        return copy

    return send, used


def front_kernel(
    attn_ref, weight_ref, residual_ref, gain_ref, extra_ref, mixed_ref, all_ref,
    made, core_in, x_out, x_in, own, own_sem, send_sems, recv_sems,
):
    at = Place()
    z, y, x, c = at.z, at.y, at.x, at.c
    at.enter()
    send, used = sender(send_sems, recv_sems)
    rows, width = residual_ref.shape
    step = 512
    for start in range(0, width, step):
        part = jnp.dot(
            attn_ref[...], weight_ref[:, start : start + step], preferred_element_type=jnp.float32
        )
        for shard in range(4):
            made[shard, :, start : start + step] = part[
                shard * rows : (shard + 1) * rows
            ].astype(jnp.bfloat16)
    to_core_far = send(made.at[(1 - x) * 2 + 1 - c], core_in.at[0], at.core_peer)
    to_core_near = send(made.at[x * 2 + 1 - c], core_in.at[1], at.core_peer)
    to_core_far.wait_recv()
    x_out[...] = (
        made[(1 - x) * 2 + c].astype(jnp.float32) + core_in[0].astype(jnp.float32)
    ).astype(jnp.bfloat16)
    to_x = send(x_out, x_in, at.x_peer)
    to_core_near.wait_recv()
    mixed = (
        residual_ref[...].astype(jnp.float32)
        + made[x * 2 + c].astype(jnp.float32)
        + core_in[1].astype(jnp.float32)
    )
    to_x.wait_recv()
    mixed = mixed + x_in[...].astype(jnp.float32)
    mixed_ref[...] = mixed
    mean_sq = jnp.mean(mixed * mixed, axis=-1, keepdims=True)
    own[:, :width] = (mixed * lax.rsqrt(mean_sq + 1e-06) * gain_ref[...]).astype(jnp.bfloat16)
    own[:, width:] = extra_ref[...]

    half = width // 2
    columns = [pl.ds(0, half), pl.ds(half, half + EXTRA)]
    first_peer, second_peer = [at.y_peer, at.x_peer], [at.x_peer, at.y_peer]

    def block(h, zs, first_other, second_other):
        ys = first_other if h == 0 else second_other
        xs = second_other if h == 0 else first_other
        return all_ref.at[zs, 1 - y if ys else y, 1 - x if xs else x, c, :, columns[h]]

    def source(j):
        return (z + 4 - j) % 4

    z_copies, first_copies, second_copies, core_copies = {}, {}, {}, []
    for j in (1, 2, 3):
        for h in (0, 1):
            z_copies[h, j] = send(own.at[:, columns[h]], block(h, z, 0, 0), at.z_peers[j])
    keep = pltpu.make_async_copy(own, all_ref.at[z, y, x, c], own_sem)
    keep.start()
    for j in range(4):
        for h in (0, 1):
            mine = block(h, source(j), 0, 0)
            if j:
                z_copies[h, j].wait_recv()
            held = mine if j else own.at[:, columns[h]]
            first_copies[h, j] = send(held, mine, first_peer[h])
            second_copies[h, j, 0] = send(held, mine, second_peer[h])
            core_copies.append(send(held, mine, at.core_peer))
    for j in range(4):
        for h in (0, 1):
            first_copies[h, j].wait_recv()
            mine = block(h, source(j), 1, 0)
            second_copies[h, j, 1] = send(mine, mine, second_peer[h])
            core_copies.append(send(mine, mine, at.core_peer))
    for other in (0, 1):
        for j in range(4):
            for h in (0, 1):
                second_copies[h, j, other].wait_recv()
                mine = block(h, source(j), other, 1)
                core_copies.append(send(mine, mine, at.core_peer))
    for copy in core_copies:
        copy.wait_recv()
    for copy in used:
        copy.wait_send()
    keep.wait()


FRONT_COPIES = 3 + 2 * (3 + 4 + 8 + 16)


def front(attn_out, out_weight, residual, norm_gain, extra):
    rows, width = residual.shape
    vmem = pl.BlockSpec(memory_space=pltpu.VMEM)
    return pl.pallas_call(
        front_kernel,
        out_shape=(
            jax.ShapeDtypeStruct((rows, width), jnp.float32),
            jax.ShapeDtypeStruct((4, 2, 2, 2, rows, width + EXTRA), jnp.bfloat16),
        ),
        in_specs=[vmem] * 5,
        out_specs=(vmem, pl.BlockSpec(memory_space=pl.ANY)),
        scratch_shapes=[
            pltpu.VMEM((4, rows, width), jnp.bfloat16),
            pltpu.VMEM((2, rows, width), jnp.bfloat16),
            pltpu.VMEM((rows, width), jnp.bfloat16),
            pltpu.VMEM((rows, width), jnp.bfloat16),
            pltpu.VMEM((rows, width + EXTRA), jnp.bfloat16),
            pltpu.SemaphoreType.DMA,
            pltpu.SemaphoreType.DMA((FRONT_COPIES,)),
            pltpu.SemaphoreType.DMA((FRONT_COPIES,)),
        ],
        compiler_params=pltpu.CompilerParams(
            collective_id=0, has_side_effects=True, vmem_limit_bytes=12 << 20
        ),
        name="front",
    )(attn_out, out_weight, residual, norm_gain.reshape(1, width), extra)


def back_kernel(
    partial_ref, mixed_ref, gain_ref, pages_ref, chosen_ref, new_ref, normed_ref, arrived_ref,
    pages_in, core_in, first_out, first_in, second_out, second_in, z_out, z_in, send_sems, recv_sems,
):
    at = Place()
    z, y, x, c = at.z, at.y, at.x, at.c
    at.enter()
    send, used = sender(send_sems, recv_sems)
    rows, width = mixed_ref.shape
    half = width // 2
    columns = [pl.ds(0, half), pl.ds(half, half)]
    first_peer, second_peer = [at.x_peer, at.y_peer], [at.y_peer, at.x_peer]
    order = (1, 2, 3, 0)

    def block(h, j, first_other, second_other, core):
        xs = first_other if h == 0 else second_other
        ys = second_other if h == 0 else first_other
        return (
            (z + j) % 4, 1 - y if ys else y, 1 - x if xs else x, core, slice(None), columns[h],
        )

    def wide(value):
        return value.astype(jnp.float32)

    core_copies, first_copies, second_copies, z_copies = {}, {}, {}, {}
    page_z = [
        send(pages_ref, pages_in.at[z, y], at.z_peers[j]) if j else None for j in range(4)
    ]
    pages_in[z, y] = pages_ref[...]
    for first_other in (1, 0):
        for j in order:
            for h in (0, 1):
                for second_other in (1, 0):
                    slot = (h, first_other, j, second_other)
                    core_copies[slot] = send(
                        partial_ref.at[block(h, j, first_other, second_other, 1 - c)],
                        core_in.at[slot],
                        at.core_peer,
                    )
    for j in order:
        for h in (0, 1):
            for second_other in (1, 0):
                core_copies[h, 1, j, second_other].wait_recv()
                first_out[h, j, second_other] = (
                    wide(partial_ref[block(h, j, 1, second_other, c)])
                    + wide(core_in[h, 1, j, second_other])
                ).astype(jnp.bfloat16)
                slot = (h, j, second_other)
                first_copies[slot] = send(first_out.at[slot], first_in.at[slot], first_peer[h])

    def gathered(h, j, second_other):
        core_copies[h, 0, j, second_other].wait_recv()
        first_copies[h, j, second_other].wait_recv()
        return (
            wide(partial_ref[block(h, j, 0, second_other, c)])
            + wide(core_in[h, 0, j, second_other])
            + wide(first_in[h, j, second_other])
        )

    for j in order:
        for h in (0, 1):
            second_out[h, j] = gathered(h, j, 1).astype(jnp.bfloat16)
            second_copies[h, j] = send(second_out.at[h, j], second_in.at[h, j], second_peer[h])
    page_y = []
    for j in range(4):
        if j:
            page_z[j].wait_recv()
        spot = pages_in.at[(z + 4 - j) % 4, y]
        page_y.append(send(spot if j else pages_ref, spot, at.y_peer))
    for j in order:
        for h in (0, 1):
            total = gathered(h, j, 0)
            second_copies[h, j].wait_recv()
            total = total + wide(second_in[h, j])
            if j:
                z_out[h, j - 1] = total.astype(jnp.bfloat16)
                z_copies[h, j] = send(z_out.at[h, j - 1], z_in.at[h, j - 1], at.z_peers[j])
            else:
                mixed_half = mixed_ref[:, columns[h]] + total
                for k in (1, 2, 3):
                    z_copies[h, k].wait_recv()
                    mixed_half = mixed_half + wide(z_in[h, k - 1])
                if h == 0:
                    left = mixed_half
    right = mixed_half
    total_sq = jnp.sum(left * left, axis=-1, keepdims=True) + jnp.sum(
        right * right, axis=-1, keepdims=True
    )
    scale = lax.rsqrt(total_sq / width + 1e-06)
    for h, value in enumerate((left, right)):
        new_ref[:, columns[h]] = value.astype(jnp.bfloat16)
        normed_ref[:, columns[h]] = (value * scale * gain_ref[:, columns[h]]).astype(jnp.bfloat16)
    for copy in page_y:
        copy.wait_recv()
    for slot in range(pages_ref.shape[0]):
        found = jnp.zeros(pages_ref.shape[1:], jnp.float32)
        for zs in range(4):
            for ys in (0, 1):
                held = wide(pages_in[zs, ys, slot])
                found = found + jnp.where(chosen_ref[zs, ys, slot] > 0, held, 0.0)
        arrived_ref[slot] = found.astype(jnp.bfloat16)
    for copy in used:
        copy.wait_send()


BACK_COPIES = 2 * (16 + 8 + 4 + 3) + 7


def back(partial, mixed, final_gain, pages, chosen):
    rows, width = mixed.shape
    half = width // 2
    vmem = pl.BlockSpec(memory_space=pltpu.VMEM)
    blocks = lambda *lead: pltpu.VMEM(lead + (rows, half), jnp.bfloat16)
    return pl.pallas_call(
        back_kernel,
        out_shape=(jax.ShapeDtypeStruct((rows, width), jnp.bfloat16),) * 2
        + (jax.ShapeDtypeStruct(pages.shape, jnp.bfloat16),),
        in_specs=[vmem] * 5,
        out_specs=(vmem,) * 3,
        scratch_shapes=[
            pltpu.VMEM((4, 2) + pages.shape, jnp.bfloat16),
            blocks(2, 2, 4, 2),
            blocks(2, 4, 2),
            blocks(2, 4, 2),
            blocks(2, 4),
            blocks(2, 4),
            blocks(2, 3),
            blocks(2, 3),
            pltpu.SemaphoreType.DMA((BACK_COPIES,)),
            pltpu.SemaphoreType.DMA((BACK_COPIES,)),
        ],
        compiler_params=pltpu.CompilerParams(
            collective_id=1, has_side_effects=True, vmem_limit_bytes=20 << 20
        ),
        name="back",
    )(partial, mixed, final_gain.reshape(1, width), pages, chosen)

def dispatch_kernel(rows, top_count, all_ref, router_ref, named_ref, slots_ref, combine_ref):
    width = router_ref.shape[0]
    block = all_ref.shape[1]
    span = router_ref.shape[1]
    lanes = slots_ref.shape[2]
    tokens = all_ref[0, :, :width]
    tail = all_ref[0, :, width:].astype(jnp.float32)
    named = named_ref[...]
    hits = jnp.zeros((block, span), jnp.float32)
    for k in range(top_count):
        hits = hits + jnp.where(tail[:, k : k + 1] == named, 1.0, 0.0)
    later = lax.broadcasted_iota(jnp.int32, (block, block), 0)
    sooner = lax.broadcasted_iota(jnp.int32, (block, block), 1)
    before = (later > sooner) & (later // rows == sooner // rows)
    rank = jnp.dot(
        jnp.where(before, 1.0, 0.0).astype(jnp.bfloat16),
        hits.astype(jnp.bfloat16),
        preferred_element_type=jnp.float32,
    )
    owner = lax.broadcasted_iota(jnp.int32, (block, span), 0) // rows
    slot = lax.broadcasted_iota(jnp.int32, (block, span), 1) % lanes
    wanted = (slot - owner * CAP).astype(jnp.float32)
    table = jnp.where((hits > 0) & (rank == wanted), 1.0, 0.0)
    logits = jnp.dot(tokens, router_ref[...], preferred_element_type=jnp.float32)
    combine_ref[0] = (table * jax.nn.sigmoid(logits)).astype(jnp.bfloat16)
    placed = lax.dot_general(
        table.astype(jnp.bfloat16),
        tokens,
        (((0,), (0,)), ((), ())),
        preferred_element_type=jnp.float32,
    ).astype(jnp.bfloat16)
    for e in range(slots_ref.shape[0]):
        slots_ref[e, 0] = placed[e * lanes : (e + 1) * lanes]


def dispatch(everything, router_slots, named, local_experts, rows, top_count):
    groups, block, wide = everything.shape
    width, span = router_slots.shape
    lanes = span // local_experts
    return pl.pallas_call(
        lambda *refs: dispatch_kernel(rows, top_count, *refs),
        grid=(groups,),
        out_shape=(
            jax.ShapeDtypeStruct((local_experts, groups, lanes, width), jnp.bfloat16),
            jax.ShapeDtypeStruct((groups, block, span), jnp.bfloat16),
        ),
        in_specs=[
            pl.BlockSpec((1, block, wide), lambda b: (b, 0, 0)),
            pl.BlockSpec((width, span), lambda b: (0, 0)),
            pl.BlockSpec((1, span), lambda b: (0, 0)),
        ],
        out_specs=(
            pl.BlockSpec((local_experts, 1, lanes, width), lambda b: (0, b, 0, 0)),
            pl.BlockSpec((1, block, span), lambda b: (b, 0, 0)),
        ),
        compiler_params=pltpu.CompilerParams(vmem_limit_bytes=50 << 20),
        name="dispatch",
    )(everything, router_slots, named)


def finish_kernel(experts, groups, paired_ref, down_ref, combine_ref, out_ref, held):
    step = pl.program_id(0)
    lanes = held.shape[1] // experts

    @pl.when(step < experts)
    def _():
        gate, up = paired_ref[0, 0], paired_ref[0, 1]
        hidden = (gate / (1.0 + jnp.exp(-gate)) * up).astype(jnp.bfloat16)
        made = jnp.dot(hidden, down_ref[0], preferred_element_type=jnp.float32)
        spot = pl.ds(pl.multiple_of(step * lanes, lanes), lanes)
        for b in range(groups):
            held[b, spot, :] = made[b * lanes : (b + 1) * lanes].astype(jnp.bfloat16)

    @pl.when(step >= experts)
    def _():
        out_ref[0] = jnp.dot(
            combine_ref[0], held[step - experts], preferred_element_type=jnp.float32
        ).astype(jnp.bfloat16)


def finish(paired, down_weight, combine):
    experts, _, slots, units = paired.shape
    groups, block, span = combine.shape
    width = down_weight.shape[2]
    expert = lambda i: jnp.minimum(i, experts - 1)
    group = lambda i: jnp.maximum(i - experts, 0)
    return pl.pallas_call(
        lambda *refs: finish_kernel(experts, groups, *refs),
        grid=(experts + groups,),
        out_shape=jax.ShapeDtypeStruct((groups, block, width), jnp.bfloat16),
        in_specs=[
            pl.BlockSpec((1, 2, slots, units), lambda i: (expert(i), 0, 0, 0)),
            pl.BlockSpec((1, units, width), lambda i: (expert(i), 0, 0)),
            pl.BlockSpec((1, block, span), lambda i: (group(i), 0, 0)),
        ],
        out_specs=pl.BlockSpec((1, block, width), lambda i: (group(i), 0, 0)),
        scratch_shapes=[pltpu.VMEM((groups, span, width), jnp.bfloat16)],
        compiler_params=pltpu.CompilerParams(vmem_limit_bytes=24 << 20),
        name="finish",
    )(paired, down_weight, combine)


def migrate(kv_pages, page_pick, destination):
    groups = lax.axis_size("dp")
    chosen_pages = kv_pages[page_pick[0]]
    owners = jnp.arange(groups, dtype=jnp.int32)[:, None] == destination[0][None, :]
    outgoing = jnp.where(
        owners[:, :, None, None, None], chosen_pages[None], jnp.zeros((), kv_pages.dtype)
    )
    incoming = lax.all_to_all(outgoing, "dp", split_axis=0, concat_axis=0, tiled=True)
    return jnp.sum(incoming, axis=0)


def local_slots(routes_all, first, local_experts, groups, shards, rows):
    hits = jnp.any(
        routes_all[:, :, None] == first + jnp.arange(local_experts, dtype=jnp.int32), axis=1
    )
    hits = hits.reshape(groups, shards * rows, local_experts)
    token = jnp.arange(shards * rows, dtype=jnp.int32)
    before = (token[:, None] > token[None, :]) & (
        token[:, None] // rows == token[None, :] // rows
    )
    rank = jnp.einsum(
        "ut,bte->bue",
        before.astype(jnp.bfloat16),
        hits.astype(jnp.bfloat16),
        preferred_element_type=jnp.float32,
    ).astype(jnp.int32)
    within = (token // rows * CAP)[None, :, None] + rank
    within = jnp.where(hits, within, -1)
    slots = jnp.arange(shards * CAP, dtype=jnp.int32)
    table = within[:, :, :, None] == slots
    return table.reshape(groups, shards * rows, local_experts * shards * CAP)


def per_device(
    attn_out,
    residual,
    out_weight,
    norm_gain,
    router_weight,
    routes,
    gate_up,
    down_weight,
    final_gain,
    kv_pages,
    page_pick,
    destination,
):
    groups = lax.axis_size("dp")
    shards = lax.axis_size("tensor")
    rows, width = residual.shape
    local_experts = gate_up.shape[0]
    first = lax.axis_index("dp") * local_experts
    grid = groups == 8 and shards == 4
    if grid:
        top_count = routes.shape[1]
        extra = jnp.concatenate(
            [routes, jnp.broadcast_to(destination, (rows, destination.shape[1]))], axis=1
        ).astype(jnp.bfloat16)
        extra = jnp.pad(extra, ((0, 0), (0, EXTRA - extra.shape[1])))
        pages = kv_pages[page_pick[0]]
        moved = pages.reshape(pages.shape[0], pages.shape[1], -1)
        local_router = lax.dynamic_slice_in_dim(router_weight, first, local_experts, axis=1)
        router_slots = jnp.repeat(local_router, shards * CAP, axis=1)
        named = first + jnp.arange(local_experts * shards * CAP) // (shards * CAP)
        mixed_sum, everything = front(attn_out, out_weight, residual, norm_gain, extra)
        owners = everything[:, :, 0, 0, 0, width + top_count : width + top_count + 2]
        chosen = (owners.astype(jnp.int32) == lax.axis_index("dp")).astype(jnp.float32)
        chosen = jnp.broadcast_to(chosen[..., None, None], chosen.shape + (1, moved.shape[2]))
        everything = everything.reshape(groups, shards * rows, width + EXTRA)
        slotted, combine = dispatch(
            everything,
            router_slots,
            named.astype(jnp.float32).reshape(1, -1),
            local_experts,
            rows,
            top_count,
        )
        paired = jnp.einsum(
            "emd,edgf->egmf",
            slotted.reshape(local_experts, -1, width),
            gate_up,
            preferred_element_type=jnp.float32,
        )
        partial = finish(paired, down_weight, combine)
        new_residual, normed, arrived = back(
            partial.reshape(4, 2, 2, 2, rows, width), mixed_sum, final_gain, moved, chosen
        )
        return (new_residual, normed, arrived.reshape(pages.shape))
    else:
        arrived = migrate(kv_pages, page_pick, destination)
        routes_all = lax.all_gather(routes, ("dp", "tensor"), axis=0, tiled=True)
        projected = lax.psum_scatter(
            jnp.dot(attn_out, out_weight, preferred_element_type=jnp.float32).astype(
                jnp.bfloat16
            ),
            "tensor",
            scatter_dimension=0,
            tiled=True,
        ).astype(jnp.float32)
        mixed_sum = residual.astype(jnp.float32) + projected
        normed_in = rms_scale(mixed_sum, norm_gain).astype(jnp.bfloat16)
        tokens = lax.all_gather(normed_in, ("dp", "tensor"), axis=0, tiled=True)
    table = local_slots(routes_all, first, local_experts, groups, shards, rows)
    local_router = lax.dynamic_slice_in_dim(router_weight, first, local_experts, axis=1)
    logits = jnp.dot(tokens, local_router, preferred_element_type=jnp.float32)
    gates = jax.nn.sigmoid(logits).astype(jnp.bfloat16)
    tokens = tokens.reshape(groups, shards * rows, width)
    gates = jnp.repeat(
        gates.reshape(groups, shards * rows, local_experts), shards * CAP, axis=2
    )
    placement = table.astype(jnp.bfloat16)
    combine = jnp.where(table, gates, jnp.zeros((), jnp.bfloat16))
    slotted = jnp.einsum(
        "bts,btd->bsd", placement, tokens, preferred_element_type=jnp.float32
    ).astype(jnp.bfloat16)
    slotted = slotted.reshape(groups, local_experts, shards * CAP, width)
    paired = jnp.einsum(
        "becd,edgf->becgf", slotted, gate_up, preferred_element_type=jnp.float32
    )
    hidden = (jax.nn.silu(paired[..., 0, :]) * paired[..., 1, :]).astype(jnp.bfloat16)
    expert_out = jnp.einsum(
        "becf,efd->becd", hidden, down_weight, preferred_element_type=jnp.float32
    ).astype(jnp.bfloat16)
    expert_out = expert_out.reshape(groups, local_experts * shards * CAP, width)
    partial = jnp.einsum(
        "bts,bsd->btd", combine, expert_out, preferred_element_type=jnp.float32
    ).astype(jnp.bfloat16)
    moe_sum = lax.psum_scatter(
        partial.reshape(groups * shards * rows, width),
        ("dp", "tensor"),
        scatter_dimension=0,
        tiled=True,
    ).astype(jnp.float32)
    combined = mixed_sum + moe_sum
    new_residual = combined.astype(jnp.bfloat16)
    normed = rms_scale(combined, final_gain).astype(jnp.bfloat16)
    return (new_residual, normed, arrived)


def solution(mesh):
    in_specs = (
        P("dp", "tensor"),
        P(("dp", "tensor"), None),
        P("tensor", None),
        P(),
        P(),
        P(("dp", "tensor"), None),
        P("dp", None, None, "tensor"),
        P("dp", "tensor", None),
        P(),
        P("dp", None, "tensor", None),
        P("dp", None),
        P("dp", None),
    )
    out_specs = (
        P(("dp", "tensor"), None),
        P(("dp", "tensor"), None),
        P("dp", None, "tensor", None),
    )
    return jax.shard_map(
        per_device, mesh=mesh, in_specs=in_specs, out_specs=out_specs, check_vma=False
    )
```
